32 devices in a mesh: row: 8 (over y, x, core), col: 4 (over z).
Axes of the slice: x: 2, y: 2, z: 4, core: 2. Of those that a mesh axis runs over, the one named last changes fastest.
Arguments:
- tiles: bfloat16 [8192, 128, 128], P(('row', 'col'))
- tile_src: int32 [8192], P(('row', 'col')), may hold values from 0 to 15
- tile_slot: int32 [8192], P(('row', 'col')), may hold values from 0 to 127
- slot_block: int32 [4096], P(('row', 'col')), may hold values from 0 to 15
- out_degree: int32 [65536], P(('row', 'col')), may hold values from 512 to 2047
- good_seeds: int32 [128, 4096], P(None, ('row', 'col')), may hold values from 0 to 65535, as said below
- spam_cores: int32 [128, 2048], P(None, ('row', 'col')), may hold values from 0 to 65535, as said below
Outputs:
- trust: float32 [65536, 128], P(('row', 'col'))
- distrust: float32 [65536, 128], P(('row', 'col'))
The draws below stay inside these ranges and needn't reach their ends.
Inputs may be any that keep to these rules, and one draw needn't show every extreme that they name: `tile_slot`: slot s of a device belongs to the peer with index s // 4 along row+col. `slot_block`: entry p * 128 + s is the local index, among the 16 blocks held by peer s // 4, of the target block of slot s of device p. `good_seeds`: entries j * 128 to (j + 1) * 128 - 1 of each column's list are hosts of device j, from j * 2048 to (j + 1) * 2048 - 1. `spam_cores`: entries j * 64 to (j + 1) * 64 - 1 of each column's list are hosts of device j, from j * 2048 to (j + 1) * 2048 - 1.
All inputs are finite; a program needn't handle non-finite values.
Results may differ from the reference program's by a relative error of at most 0.0003.
Values may be sent and summed in bfloat16 or wider, within the bound.
A program may use at most 128 MiB of HBM per device.

```python
import math
import jax
import jax.numpy as jnp
import numpy as np
from jax import lax

BS = 128
S = 128
BLK_DEV = 16
TILES_DEV = 256
SLOTS_DEV = 128
TRUST_ITERS = 2
ANTI_ITERS = 2
CAP = 4
HOSTS_DEV = 2048
NB = 512
HOSTS = 65536
NTILES = 8192
SLOTS = 4096
GOOD_DEV = 128
K_GOOD = 4096
SPAM_DEV = 64
K_SPAM = 2048
N_ROW = 8
N_COL = 4


def draw_tiles(key, part):
    first, second, third = jax.random.split(key, 3)
    base = 4.6 * jnp.exp(jax.random.uniform(first, (NTILES, BS, BS), jnp.float32, math.log(0.0001), 0.0))
    lower, upper = (0.3, 3.0)
    row_scale = jnp.exp(jax.random.uniform(second, (NTILES, BS, 1), jnp.float32, math.log(lower), math.log(upper)))
    column_scale = jnp.exp(jax.random.uniform(third, (NTILES, 1, BS), jnp.float32, math.log(lower), math.log(upper)))
    return (base * row_scale * column_scale).astype(jnp.bfloat16)


def local_hosts(key, per_device, total):
    local = jax.random.randint(key, (S, total), 0, HOSTS_DEV, dtype=jnp.int32)
    owner = (jnp.arange(total, dtype=jnp.int32) // per_device).astype(jnp.int32)
    return (local + owner[None, :] * HOSTS_DEV).astype(jnp.int32)


def draw_good_seeds(key, part):
    return local_hosts(jax.random.fold_in(key, 11), GOOD_DEV, K_GOOD)


def draw_spam_cores(key, part):
    return local_hosts(jax.random.fold_in(key, 23), SPAM_DEV, K_SPAM)


def plant(values, key, least, high):
    longest = values.shape.index(max(values.shape))
    spots = []
    for shift in (0, 1):
        where = [jax.random.randint(jax.random.fold_in(key, axis), (), 0, length) for axis, length in enumerate(values.shape)]
        where[longest] = (where[longest] + shift) % values.shape[longest]
        spots.append(tuple(where))
    return values.at[spots[0]].set(least).at[spots[1]].set(high)


def rank_table(count, lean):
    loads = [(1 << 20) // math.isqrt(grade ** lean) + 1 for grade in range(1, count + 1)]
    deviation = 1 + sum(loads) // (1 << 30)
    return np.cumsum(np.array([max(1, weight // deviation) for weight in loads]))


def ranked_ids(stream_key, shape, amount, slope):
    grid = rank_table(amount, slope)
    pick = jax.random.randint(jax.random.fold_in(stream_key, 1), shape, 0, int(grid[amount - 1]))
    standing = jnp.searchsorted(jnp.asarray(grid, jnp.int32), pick, side="right")
    return jax.random.permutation(jax.random.fold_in(stream_key, 2), amount)[standing].astype(jnp.int32)


def setup_inputs(seed: int = 0) -> dict:
    key_list = jax.random.split(jax.random.key(seed), 8)
    tiles = draw_tiles(jax.random.fold_in(key_list[7], 71), 0)
    tile_src = plant(jax.random.randint(key_list[1], (NTILES,), 0, BLK_DEV), jax.random.fold_in(key_list[1], 1), 0, BLK_DEV - 1).astype(jnp.int32)
    tile_slot = plant(jax.random.randint(key_list[2], (NTILES,), 0, SLOTS_DEV), jax.random.fold_in(key_list[2], 1), 0, SLOTS_DEV - 1).astype(jnp.int32)
    slot_block = plant(ranked_ids(key_list[3], (SLOTS,), BLK_DEV, 1), jax.random.fold_in(key_list[3], 3), 0, BLK_DEV - 1).astype(jnp.int32)
    out_degree = plant(jax.random.randint(key_list[4], (HOSTS,), TILES_DEV * BS // (4 * BLK_DEV), TILES_DEV * BS // BLK_DEV), jax.random.fold_in(key_list[4], 1), TILES_DEV * BS // (4 * BLK_DEV), (TILES_DEV * BS // BLK_DEV) - 1).astype(jnp.int32)
    good_seeds = draw_good_seeds(jax.random.fold_in(key_list[7], 71), 0)
    spam_cores = draw_spam_cores(jax.random.fold_in(key_list[7], 71), 0)
    return dict(tiles=tiles, tile_src=tile_src, tile_slot=tile_slot, slot_block=slot_block, out_degree=out_degree, good_seeds=good_seeds, spam_cores=spam_cores)


def teleport(seeds, factor):
    column_index = jnp.broadcast_to(jnp.arange(S, dtype=jnp.int32)[:, None], seeds.shape)
    counts = jnp.zeros((HOSTS, S), jnp.float32).at[seeds, column_index].add(jnp.float32(1.0))
    return counts * jnp.float32(factor)


def reference(tiles, tile_src, tile_slot, slot_block, out_degree, good_seeds, spam_cores):
    devices = N_ROW * N_COL
    owner = (jnp.arange(NTILES, dtype=jnp.int32) // TILES_DEV).astype(jnp.int32)
    source_block = (owner * BLK_DEV + tile_src).astype(jnp.int32)
    global_slot = (owner * SLOTS_DEV + tile_slot).astype(jnp.int32)
    target_block = ((tile_slot // CAP) * BLK_DEV + slot_block[global_slot]).astype(jnp.int32)
    column_sums = jnp.sum(tiles, axis=1, dtype=jnp.float32)
    in_weight = 1.0 + jax.ops.segment_sum(column_sums, target_block, num_segments=NB).reshape(HOSTS)
    good_start = teleport(good_seeds, HOSTS_DEV / GOOD_DEV)
    spam_start = teleport(spam_cores, HOSTS_DEV / SPAM_DEV)
    grouped = tiles.reshape(devices, TILES_DEV, BS, BS)
    source_groups = source_block.reshape(devices, TILES_DEV)
    target_groups = target_block.reshape(devices, TILES_DEV)

    def forward(scaled):
        blocks = scaled.reshape(NB, BS, S)

        def one_group(total, group):
            weights, sources, targets = group
            products = jnp.einsum("kij,kis->kjs", weights.astype(jnp.float32), blocks[sources].astype(jnp.float32), precision=lax.Precision.HIGHEST)
            return total + jax.ops.segment_sum(products, targets, num_segments=NB), None

        total, _ = lax.scan(one_group, jnp.zeros((NB, BS, S), jnp.float32), (grouped, source_groups, target_groups))
        return total.reshape(HOSTS, S)

    def backward(share):
        blocks = share.reshape(NB, BS, S)

        def one_group(total, group):
            weights, sources, targets = group
            products = jnp.einsum("kij,kjs->kis", weights.astype(jnp.float32), blocks[targets].astype(jnp.float32), precision=lax.Precision.HIGHEST)
            return total + jax.ops.segment_sum(products, sources, num_segments=NB), None

        total, _ = lax.scan(one_group, jnp.zeros((NB, BS, S), jnp.float32), (grouped, source_groups, target_groups))
        return total.reshape(HOSTS, S)

    degree = out_degree.astype(jnp.float32)[:, None]
    trust = good_start
    for iteration in range(TRUST_ITERS):
        scaled = (trust / degree).astype(jnp.bfloat16)
        trust = 0.85 * forward(scaled) + 0.15 * good_start
    shield = 1.0 / (1.0 + trust)
    distrust = spam_start
    for iteration in range(ANTI_ITERS):
        share = (shield * distrust / in_weight[:, None]).astype(jnp.bfloat16)
        distrust = 0.85 * backward(share) + 0.15 * spam_start
    return trust, distrust
```

```python
import functools

import jax
import jax.numpy as jnp
from jax import lax
from jax.experimental import pallas as pl
from jax.experimental.pallas import tpu as pltpu
from jax.sharding import PartitionSpec as P

AXES = ("row", "col")
VM = pl.BlockSpec(memory_space=pltpu.VMEM)
SM = pl.BlockSpec(memory_space=pltpu.SMEM)
F32 = jnp.float32
BF16 = jnp.bfloat16
WORD = 15


def seed_kernel(columns, good_seeds_ref, spam_cores_ref, good_ref, spam_ref):
    blocks, seeds, size = good_ref.shape
    hosts = blocks * size
    base = (lax.axis_index("row") * columns + lax.axis_index("col")) * hosts
    for source, target in ((good_seeds_ref, good_ref), (spam_cores_ref, spam_ref)):
        count = source.shape[1]
        factor = F32(hosts / count)
        block_iota = lax.broadcasted_iota(jnp.int32, (blocks, count), 0) * size
        lane_iota = lax.broadcasted_iota(jnp.int32, (size, count), 0)

        def one(s, _):
            local = source[pl.ds(s, 1), :] - base
            shifted = local - block_iota
            inside = jnp.where((shifted >= 0) & (shifted < size), F32(1), F32(0)).astype(BF16)
            start = jnp.max(jnp.where(local >= block_iota, block_iota, 0), axis=0, keepdims=True)
            lane = jnp.where(lane_iota == local - start, F32(1), F32(0)).astype(BF16)
            counts = lax.dot_general(
                inside, lane, (((1,), (1,)), ((), ())), preferred_element_type=F32
            )
            for b in range(blocks):
                target[b, pl.ds(s, 1), :] = counts[b : b + 1, :] * factor
            return 0

        lax.fori_loop(0, seeds, one, 0, unroll=4)


def exponent_of(peak):
    return jnp.floor(jnp.log2(jnp.maximum(peak, F32(2.0**-100)))) + F32(1)


def to_words(value):
    return jnp.clip(jnp.floor(value + F32(0.5)), F32(-32767), F32(32767))


def pack(first, cap, acc, out_ref):
    peers = out_ref.shape[0]
    size = acc.shape[2]
    tail = out_ref.shape[1] - cap * size

    def one(p, _):
        exps, cols = [], []
        for c in range(cap):
            n = p * cap + c
            value = acc[n, :size, :]
            e = exponent_of(jnp.max(jnp.abs(value), axis=0, keepdims=True))
            out_ref[p, c * size : (c + 1) * size, :] = to_words(value * jnp.exp2(WORD - e)).astype(
                jnp.int32
            ).astype(jnp.int16)
            exps.append(e)
            if first:
                col = acc[n, size : size + 8, :][:1, :]
                f = exponent_of(jnp.abs(col))
                scaled = col * jnp.exp2(WORD - f)
                high = to_words(scaled)
                cols += [f, high, to_words((scaled - high) * F32(2.0**WORD))]
        rows = exps + cols
        if tail > len(rows):
            rows.append(jnp.zeros((tail - len(rows), size), F32))
        out_ref[p, cap * size :, :] = jnp.concatenate(rows, axis=0).astype(jnp.int32).astype(jnp.int16)
        return 0

    lax.fori_loop(0, peers, one, 0)


def unpack(cap, ids_ref, arrived_ref, inflow, weight):
    peers = arrived_ref.shape[0]
    size = inflow.shape[2]
    inflow[...] = jnp.zeros_like(inflow)
    if weight is not None:
        weight[...] = jnp.ones_like(weight)

    def one(p, _):
        rows = arrived_ref[p, cap * size :, :].astype(jnp.int32).astype(F32)
        for c in range(cap):
            b = ids_ref[p * cap + c]
            value = arrived_ref[p, c * size : (c + 1) * size, :].astype(jnp.int32).astype(F32)
            inflow[b] += value * jnp.exp2(rows[c : c + 1, :] - WORD)
            if weight is not None:
                at = cap + 3 * c
                f, high, low = (rows[at + i : at + i + 1, :] for i in range(3))
                weight[b] += (high + low * F32(2.0**-WORD)) * jnp.exp2(f - WORD)
        return 0

    lax.fori_loop(0, peers, one, 0)


def push_kernel(first, cap, *refs):
    if first:
        src_ref, slot_ref, good_ref, degree_ref, tiles_ref, out_ref, acc, scaled = refs
    else:
        (src_ref, slot_ref, ids_ref, arrived_ref, good_ref, degree_ref, tiles_ref,
         out_ref, weight_ref, acc, scaled, inflow) = refs
    step = pl.program_id(0)
    blocks, seeds, size = good_ref.shape
    per_step = tiles_ref.shape[0]

    @pl.when(step == 0)
    def _():
        acc[...] = jnp.zeros_like(acc)
        if not first:
            unpack(cap, ids_ref, arrived_ref, inflow, weight_ref)

        def one(b, _):
            degree = degree_ref[b].astype(F32)
            trust = good_ref[b]
            if not first:
                trust = F32(0.85) * inflow[b] + F32(0.15) * trust
            scaled[b, :seeds, :] = (trust / degree).astype(BF16)
            if first:
                scaled[b, seeds:, :] = jnp.ones((scaled.shape[1] - seeds, size), BF16)
            return 0

        lax.fori_loop(0, blocks, one, 0)

    def one(k, _):
        n = step * per_step + k
        acc[slot_ref[n]] += jnp.dot(scaled[src_ref[n]], tiles_ref[k], preferred_element_type=F32)
        return 0

    lax.fori_loop(0, per_step, one, 0, unroll=4)

    @pl.when(step == pl.num_programs(0) - 1)
    def _():
        pack(first, cap, acc, out_ref)


def shares(ids_ref, shield_ref, weight_ref, start_of, share, asked_ref):
    def one(b, _):
        share[b] = (shield_ref[b] * start_of(b) / weight_ref[b]).astype(BF16)
        return 0

    lax.fori_loop(0, share.shape[0], one, 0)

    def ask(n, _):
        asked_ref[n] = share[ids_ref[n]]
        return 0

    lax.fori_loop(0, asked_ref.shape[0], ask, 0)


def trust_kernel(cap, ids_ref, arrived_ref, good_ref, spam_ref, weight_ref,
                 trust_ref, shield_ref, asked_ref, inflow, share):
    unpack(cap, ids_ref, arrived_ref, inflow, None)
    size = inflow.shape[2]

    def one(b, _):
        trust = F32(0.85) * inflow[b] + F32(0.15) * good_ref[b]
        trust_ref[pl.ds(pl.multiple_of(b * size, size), size), :] = jnp.transpose(trust)
        shield_ref[b] = F32(1) / (F32(1) + trust)
        return 0

    lax.fori_loop(0, inflow.shape[0], one, 0)
    shares(ids_ref, shield_ref, weight_ref, lambda b: spam_ref[b], share, asked_ref)


def pull_kernel(last, *refs):
    if last:
        src_ref, slot_ref, fetched_ref, spam_ref, tiles_ref, out_ref, acc = refs
    else:
        (src_ref, slot_ref, ids_ref, fetched_ref, spam_ref, shield_ref, weight_ref, tiles_ref,
         out_ref, acc, share) = refs
    step = pl.program_id(0)
    per_step = tiles_ref.shape[0]
    size = acc.shape[2]

    @pl.when(step == 0)
    def _():
        acc[...] = jnp.zeros_like(acc)

    def one(k, _):
        n = step * per_step + k
        acc[src_ref[n]] += lax.dot_general(
            fetched_ref[slot_ref[n]], tiles_ref[k], (((1,), (1,)), ((), ())),
            preferred_element_type=F32,
        )
        return 0

    lax.fori_loop(0, per_step, one, 0, unroll=4)

    @pl.when(step == pl.num_programs(0) - 1)
    def _():
        def distrust(b):
            return F32(0.85) * acc[b] + F32(0.15) * spam_ref[b]

        if last:
            def one(b, _):
                out_ref[pl.ds(pl.multiple_of(b * size, size), size), :] = jnp.transpose(distrust(b))
                return 0

            lax.fori_loop(0, acc.shape[0], one, 0)
        else:
            shares(ids_ref, shield_ref, weight_ref, distrust, share, out_ref)


def body(columns, tiles, tile_src, tile_slot, slot_block, out_degree, good_seeds, spam_cores):
    tile_count, size, _ = tiles.shape
    hosts = out_degree.shape[0]
    blocks = hosts // size
    seeds = good_seeds.shape[0]
    slots = slot_block.shape[0]
    peers = lax.axis_size(AXES)
    cap = slots // peers
    tail = -(-4 * cap // 16) * 16
    steps = 8
    shape = jax.ShapeDtypeStruct
    vector = (blocks, seeds, size)
    degree = out_degree.reshape(blocks, 1, size)

    def exchange(x):
        return lax.all_to_all(x, AXES, split_axis=0, concat_axis=0, tiled=True)

    ids = exchange(slot_block.reshape(peers, cap)).reshape(slots)
    good, spam = pl.pallas_call(
        functools.partial(seed_kernel, columns),
        out_shape=(shape(vector, F32), shape(vector, F32)),
        in_specs=[VM, VM],
        out_specs=(VM, VM),
    )(good_seeds, spam_cores)

    tile_spec = pl.BlockSpec((tile_count // steps, size, size), lambda i: (i, 0, 0))
    words = shape((peers, cap * size + tail, size), jnp.int16)
    outgoing = pl.pallas_call(
        functools.partial(push_kernel, True, cap),
        grid=(steps,),
        out_shape=words,
        in_specs=[SM, SM, VM, VM, tile_spec],
        out_specs=VM,
        scratch_shapes=[
            pltpu.VMEM((slots, seeds + 16, size), F32),
            pltpu.VMEM((blocks, seeds + 16, size), BF16),
        ],
    )(tile_src, tile_slot, good, degree, tiles)
    arrived = exchange(outgoing)
    outgoing, weight = pl.pallas_call(
        functools.partial(push_kernel, False, cap),
        grid=(steps,),
        out_shape=(words, shape((blocks, 1, size), F32)),
        in_specs=[SM, SM, SM, VM, VM, VM, tile_spec],
        out_specs=(VM, VM),
        scratch_shapes=[
            pltpu.VMEM((slots, seeds, size), F32),
            pltpu.VMEM(vector, BF16),
            pltpu.VMEM(vector, F32),
        ],
    )(tile_src, tile_slot, ids, arrived, good, degree, tiles)
    arrived = exchange(outgoing)
    asked_shape = shape((slots, seeds, size), BF16)
    trust, shield, asked = pl.pallas_call(
        functools.partial(trust_kernel, cap),
        out_shape=(shape((hosts, seeds), F32), shape(vector, F32), asked_shape),
        in_specs=[SM, VM, VM, VM, VM],
        out_specs=(VM, VM, VM),
        scratch_shapes=[pltpu.VMEM(vector, F32), pltpu.VMEM(vector, BF16)],
    )(ids, arrived, good, spam, weight)
    fetched = exchange(asked)
    asked = pl.pallas_call(
        functools.partial(pull_kernel, False),
        grid=(steps,),
        out_shape=asked_shape,
        in_specs=[SM, SM, SM, VM, VM, VM, VM, tile_spec],
        out_specs=VM,
        scratch_shapes=[pltpu.VMEM(vector, F32), pltpu.VMEM(vector, BF16)],
    )(tile_src, tile_slot, ids, fetched, spam, shield, weight, tiles)
    fetched = exchange(asked)
    distrust = pl.pallas_call(
        functools.partial(pull_kernel, True),
        grid=(steps,),
        out_shape=shape((hosts, seeds), F32),
        in_specs=[SM, SM, VM, VM, tile_spec],
        out_specs=VM,
        scratch_shapes=[pltpu.VMEM(vector, F32)],
    )(tile_src, tile_slot, fetched, spam, tiles)
    return trust, distrust


def solution(mesh):
    in_specs = (
        P(AXES, None, None),
        P(AXES),
        P(AXES),
        P(AXES),
        P(AXES),
        P(None, AXES),
        P(None, AXES),
    )
    out_specs = (P(AXES, None), P(AXES, None))
    return jax.shard_map(
        functools.partial(body, mesh.shape["col"]),
        mesh=mesh, in_specs=in_specs, out_specs=out_specs, check_vma=False,
    )
```

```python
import functools

import jax
import jax.numpy as jnp
from jax import lax
from jax.experimental import pallas as pl
from jax.experimental.pallas import tpu as pltpu
from jax.sharding import PartitionSpec as P

AXES = ("row", "col")
VM = pl.BlockSpec(memory_space=pltpu.VMEM)
SM = pl.BlockSpec(memory_space=pltpu.SMEM)
F32 = jnp.float32
BF16 = jnp.bfloat16
WORD = 15
MESH = pl.DeviceIdType.MESH


def seed_kernel(columns, good_seeds_ref, spam_cores_ref, good_ref, spam_ref):
    blocks, seeds, size = good_ref.shape
    hosts = blocks * size
    base = (lax.axis_index("row") * columns + lax.axis_index("col")) * hosts
    for source, target in ((good_seeds_ref, good_ref), (spam_cores_ref, spam_ref)):
        count = source.shape[1]
        factor = F32(hosts / count)
        block_iota = lax.broadcasted_iota(jnp.int32, (blocks, count), 0) * size
        lane_iota = lax.broadcasted_iota(jnp.int32, (size, count), 0)

        def one(s, _):
            local = source[pl.ds(s, 1), :] - base
            shifted = local - block_iota
            inside = jnp.where((shifted >= 0) & (shifted < size), F32(1), F32(0)).astype(BF16)
            start = jnp.max(jnp.where(local >= block_iota, block_iota, 0), axis=0, keepdims=True)
            lane = jnp.where(lane_iota == local - start, F32(1), F32(0)).astype(BF16)
            counts = lax.dot_general(
                inside, lane, (((1,), (1,)), ((), ())), preferred_element_type=F32
            )
            for b in range(blocks):
                target[b, pl.ds(s, 1), :] = counts[b : b + 1, :] * factor
            return 0

        lax.fori_loop(0, seeds, one, 0, unroll=4)


def exponent_of(peak):
    return jnp.floor(jnp.log2(jnp.maximum(peak, F32(2.0**-100)))) + F32(1)


def to_words(value):
    return jnp.clip(jnp.floor(value + F32(0.5)), F32(-32767), F32(32767))


def pack(first, cap, acc, out_ref):
    peers = out_ref.shape[0]
    size = acc.shape[2]
    tail = out_ref.shape[1] - cap * size

    def one(p, _):
        exps, cols = [], []
        for c in range(cap):
            n = p * cap + c
            value = acc[n, :size, :]
            e = exponent_of(jnp.max(jnp.abs(value), axis=0, keepdims=True))
            out_ref[p, c * size : (c + 1) * size, :] = to_words(value * jnp.exp2(WORD - e)).astype(
                jnp.int32
            ).astype(jnp.int16)
            exps.append(e)
            if first:
                col = acc[n, size : size + 8, :][:1, :]
                f = exponent_of(jnp.abs(col))
                scaled = col * jnp.exp2(WORD - f)
                high = to_words(scaled)
                cols += [f, high, to_words((scaled - high) * F32(2.0**WORD))]
        rows = exps + cols
        if tail > len(rows):
            rows.append(jnp.zeros((tail - len(rows), size), F32))
        out_ref[p, cap * size :, :] = jnp.concatenate(rows, axis=0).astype(jnp.int32).astype(jnp.int16)
        return 0

    lax.fori_loop(0, peers, one, 0)


def unpack(cap, ids_ref, arrived_ref, inflow, weight):
    peers = arrived_ref.shape[0]
    size = inflow.shape[2]
    inflow[...] = jnp.zeros_like(inflow)
    if weight is not None:
        weight[...] = jnp.ones_like(weight)

    def one(p, _):
        rows = arrived_ref[p, cap * size :, :].astype(jnp.int32).astype(F32)
        for c in range(cap):
            b = ids_ref[p * cap + c]
            value = arrived_ref[p, c * size : (c + 1) * size, :].astype(jnp.int32).astype(F32)
            inflow[b] += value * jnp.exp2(rows[c : c + 1, :] - WORD)
            if weight is not None:
                at = cap + 3 * c
                f, high, low = (rows[at + i : at + i + 1, :] for i in range(3))
                weight[b] += (high + low * F32(2.0**-WORD)) * jnp.exp2(f - WORD)
        return 0

    lax.fori_loop(0, peers, one, 0)


def push_kernel(first, cap, *refs):
    if first:
        src_ref, slot_ref, good_ref, degree_ref, tiles_ref, out_ref, acc, scaled = refs
    else:
        (src_ref, slot_ref, ids_ref, arrived_ref, good_ref, degree_ref, tiles_ref,
         out_ref, weight_ref, acc, scaled, inflow) = refs
    step = pl.program_id(0)
    blocks, seeds, size = good_ref.shape
    per_step = tiles_ref.shape[0]

    @pl.when(step == 0)
    def _():
        acc[...] = jnp.zeros_like(acc)
        if not first:
            unpack(cap, ids_ref, arrived_ref, inflow, weight_ref)

        def one(b, _):
            degree = degree_ref[b].astype(F32)
            trust = good_ref[b]
            if not first:
                trust = F32(0.85) * inflow[b] + F32(0.15) * trust
            scaled[b, :seeds, :] = (trust / degree).astype(BF16)
            if first:
                scaled[b, seeds:, :] = jnp.ones((scaled.shape[1] - seeds, size), BF16)
            return 0

        lax.fori_loop(0, blocks, one, 0)

    def one(k, _):
        n = step * per_step + k
        acc[slot_ref[n]] += jnp.dot(scaled[src_ref[n]], tiles_ref[k], preferred_element_type=F32)
        return 0

    lax.fori_loop(0, per_step, one, 0, unroll=4)

    @pl.when(step == pl.num_programs(0) - 1)
    def _():
        pack(first, cap, acc, out_ref)


def shares(shield_ref, weight_ref, start_of, share_ref):
    def one(b, _):
        share_ref[b] = (shield_ref[b] * start_of(b) / weight_ref[b]).astype(BF16)
        return 0

    lax.fori_loop(0, share_ref.shape[0], one, 0)


def greet(devices):
    barrier = pltpu.get_barrier_semaphore()
    for device, there in devices:
        @pl.when(there)
        def _():
            pl.semaphore_signal(barrier, inc=1, device_id=device, device_id_type=MESH)
    pl.semaphore_wait(barrier, sum(jnp.where(there, 1, 0) for _, there in devices))


def fetch_kernel(rows, columns, cap, want_ref, share_ref, fetched_ref, *scratch):
    line = 2 * (columns - 1)
    held, (picked, line_send, line_recv, send, recv) = scratch[:line], scratch[line:]
    r, z = lax.axis_index("row"), lax.axis_index("col")
    others = [lax.rem(r + d, rows) for d in range(1, rows)]
    sides = (-1, 1)
    inside = {side: (z + side >= 0) & (z + side < columns) for side in sides}
    greet([((t, z), t >= 0) for t in others] + [((r, z + side), inside[side]) for side in sides])

    def place(side, d):
        return 2 * (d - 1) + (0 if side < 0 else 1)

    def pass_on(source, d, side):
        slot = place(-side, d)
        return pltpu.make_async_remote_copy(
            src_ref=source, dst_ref=held[slot],
            send_sem=line_send.at[slot], recv_sem=line_recv.at[slot],
            device_id=(r, z + side), device_id_type=MESH,
        )

    def serve(t, origin):
        return pltpu.make_async_remote_copy(
            src_ref=picked.at[t, pl.ds(origin * cap, cap)],
            dst_ref=fetched_ref.at[pl.ds((r * columns + origin) * cap, cap)],
            send_sem=send.at[t, origin], recv_sem=recv.at[r, origin],
            device_id=(t, z), device_id_type=MESH,
        )

    def spread(source, origin):
        before = None
        for t in others:
            for j in range(cap):
                picked[t, origin * cap + j] = source[want_ref[t, origin * cap + j]]
            if before is not None:
                serve(before, origin).start()
            before = t
        for j in range(cap):
            fetched_ref[(r * columns + origin) * cap + j] = source[want_ref[r, origin * cap + j]]
        serve(before, origin).start()

    for side in sides:
        @pl.when(inside[side])
        def _():
            pass_on(share_ref, 1, side).start()
    spread(share_ref, z)
    for d in range(1, columns):
        for side in sides:
            origin = z + side * d

            @pl.when((origin >= 0) & (origin < columns))
            def _():
                here = held[place(side, d)]
                pass_on(share_ref, d, -side).wait_recv()

                if d < columns - 1:
                    @pl.when(inside[-side])
                    def _():
                        pass_on(here, d + 1, -side).start()

                spread(here, origin)
    for origin in range(columns):
        for t in others:
            serve(t, origin).wait_send()
            pltpu.make_async_remote_copy(
                src_ref=picked.at[t, pl.ds(origin * cap, cap)],
                dst_ref=fetched_ref.at[pl.ds((t * columns + origin) * cap, cap)],
                send_sem=send.at[t, origin], recv_sem=recv.at[t, origin],
                device_id=(t, z), device_id_type=MESH,
            ).wait_recv()
    for d in range(columns - 1):
        for side in sides:
            origin = z - side * d

            @pl.when((origin >= 0) & (origin < columns) & inside[side])
            def _():
                pass_on(share_ref, d + 1, side).wait_send()


def trust_kernel(cap, ids_ref, arrived_ref, good_ref, spam_ref, weight_ref,
                 trust_ref, shield_ref, share_ref, inflow):
    unpack(cap, ids_ref, arrived_ref, inflow, None)
    size = inflow.shape[2]

    def one(b, _):
        trust = F32(0.85) * inflow[b] + F32(0.15) * good_ref[b]
        trust_ref[pl.ds(pl.multiple_of(b * size, size), size), :] = jnp.transpose(trust)
        shield_ref[b] = F32(1) / (F32(1) + trust)
        return 0

    lax.fori_loop(0, inflow.shape[0], one, 0)
    shares(shield_ref, weight_ref, lambda b: spam_ref[b], share_ref)


def pull_kernel(last, *refs):
    if last:
        src_ref, slot_ref, fetched_ref, spam_ref, tiles_ref, out_ref, acc = refs
    else:
        (src_ref, slot_ref, fetched_ref, spam_ref, shield_ref, weight_ref, tiles_ref,
         out_ref, acc) = refs
    step = pl.program_id(0)
    per_step = tiles_ref.shape[0]
    size = acc.shape[2]

    @pl.when(step == 0)
    def _():
        acc[...] = jnp.zeros_like(acc)

    def one(k, _):
        n = step * per_step + k
        acc[src_ref[n]] += lax.dot_general(
            fetched_ref[slot_ref[n]], tiles_ref[k], (((1,), (1,)), ((), ())),
            preferred_element_type=F32,
        )
        return 0

    lax.fori_loop(0, per_step, one, 0, unroll=4)

    @pl.when(step == pl.num_programs(0) - 1)
    def _():
        def distrust(b):
            return F32(0.85) * acc[b] + F32(0.15) * spam_ref[b]

        if last:
            def one(b, _):
                out_ref[pl.ds(pl.multiple_of(b * size, size), size), :] = jnp.transpose(distrust(b))
                return 0

            lax.fori_loop(0, acc.shape[0], one, 0)
        else:
            shares(shield_ref, weight_ref, distrust, out_ref)


def body(columns, tiles, tile_src, tile_slot, slot_block, out_degree, good_seeds, spam_cores):
    tile_count, size, _ = tiles.shape
    hosts = out_degree.shape[0]
    blocks = hosts // size
    seeds = good_seeds.shape[0]
    slots = slot_block.shape[0]
    peers = lax.axis_size(AXES)
    cap = slots // peers
    tail = -(-4 * cap // 16) * 16
    steps = 8
    shape = jax.ShapeDtypeStruct
    vector = (blocks, seeds, size)
    degree = out_degree.reshape(blocks, 1, size)

    def exchange(x):
        return lax.all_to_all(x, AXES, split_axis=0, concat_axis=0, tiled=True)

    ids = exchange(slot_block.reshape(peers, cap)).reshape(slots)
    want = lax.all_to_all(
        slot_block.reshape(peers // columns, columns * cap), "row", split_axis=0, concat_axis=0, tiled=True
    )
    good, spam = pl.pallas_call(
        functools.partial(seed_kernel, columns),
        out_shape=(shape(vector, F32), shape(vector, F32)),
        in_specs=[VM, VM],
        out_specs=(VM, VM),
    )(good_seeds, spam_cores)

    tile_spec = pl.BlockSpec((tile_count // steps, size, size), lambda i: (i, 0, 0))
    words = shape((peers, cap * size + tail, size), jnp.int16)
    outgoing = pl.pallas_call(
        functools.partial(push_kernel, True, cap),
        grid=(steps,),
        out_shape=words,
        in_specs=[SM, SM, VM, VM, tile_spec],
        out_specs=VM,
        scratch_shapes=[
            pltpu.VMEM((slots, seeds + 16, size), F32),
            pltpu.VMEM((blocks, seeds + 16, size), BF16),
        ],
    )(tile_src, tile_slot, good, degree, tiles)
    arrived = exchange(outgoing)
    outgoing, weight = pl.pallas_call(
        functools.partial(push_kernel, False, cap),
        grid=(steps,),
        out_shape=(words, shape((blocks, 1, size), F32)),
        in_specs=[SM, SM, SM, VM, VM, VM, tile_spec],
        out_specs=(VM, VM),
        scratch_shapes=[
            pltpu.VMEM((slots, seeds, size), F32),
            pltpu.VMEM(vector, BF16),
            pltpu.VMEM(vector, F32),
        ],
    )(tile_src, tile_slot, ids, arrived, good, degree, tiles)
    arrived = exchange(outgoing)
    rows = peers // columns
    fetch = pl.pallas_call(
        functools.partial(fetch_kernel, rows, columns, cap),
        out_shape=shape((slots, seeds, size), BF16),
        in_specs=[SM, VM],
        out_specs=VM,
        scratch_shapes=[
            *[pltpu.VMEM(vector, BF16)] * (2 * columns - 2),
            pltpu.VMEM((rows, columns * cap, seeds, size), BF16),
            pltpu.SemaphoreType.DMA((2 * columns - 2,)),
            pltpu.SemaphoreType.DMA((2 * columns - 2,)),
            pltpu.SemaphoreType.DMA((rows, columns)),
            pltpu.SemaphoreType.DMA((rows, columns)),
        ],
        compiler_params=pltpu.CompilerParams(collective_id=0, has_side_effects=True),
    )
    trust, shield, share = pl.pallas_call(
        functools.partial(trust_kernel, cap),
        out_shape=(shape((hosts, seeds), F32), shape(vector, F32), shape(vector, BF16)),
        in_specs=[SM, VM, VM, VM, VM],
        out_specs=(VM, VM, VM),
        scratch_shapes=[pltpu.VMEM(vector, F32)],
    )(ids, arrived, good, spam, weight)
    fetched = fetch(want, share)
    share = pl.pallas_call(
        functools.partial(pull_kernel, False),
        grid=(steps,),
        out_shape=shape(vector, BF16),
        in_specs=[SM, SM, VM, VM, VM, VM, tile_spec],
        out_specs=VM,
        scratch_shapes=[pltpu.VMEM(vector, F32)],
    )(tile_src, tile_slot, fetched, spam, shield, weight, tiles)
    fetched = fetch(want, share)
    distrust = pl.pallas_call(
        functools.partial(pull_kernel, True),
        grid=(steps,),
        out_shape=shape((hosts, seeds), F32),
        in_specs=[SM, SM, VM, VM, tile_spec],
        out_specs=VM,
        scratch_shapes=[pltpu.VMEM(vector, F32)],
    )(tile_src, tile_slot, fetched, spam, tiles)
    return trust, distrust


def solution(mesh):
    in_specs = (
        P(AXES, None, None),
        P(AXES),
        P(AXES),
        P(AXES),
        P(AXES),
        P(None, AXES),
        P(None, AXES),
    )
    out_specs = (P(AXES, None), P(AXES, None))
    return jax.shard_map(
        functools.partial(body, mesh.shape["col"]),
        mesh=mesh, in_specs=in_specs, out_specs=out_specs, check_vma=False,
    )
```

```python
import functools

import jax
import jax.numpy as jnp
from jax import lax
from jax.experimental import pallas as pl
from jax.experimental.pallas import tpu as pltpu
from jax.sharding import PartitionSpec as P

AXES = ("row", "col")
VM = pl.BlockSpec(memory_space=pltpu.VMEM)
SM = pl.BlockSpec(memory_space=pltpu.SMEM)
F32 = jnp.float32
BF16 = jnp.bfloat16
WORD = 15
MESH = pl.DeviceIdType.MESH


def seed_kernel(columns, good_seeds_ref, spam_cores_ref, good_ref, spam_ref):
    blocks, seeds, size = good_ref.shape
    hosts = blocks * size
    base = (lax.axis_index("row") * columns + lax.axis_index("col")) * hosts
    for source, target in ((good_seeds_ref, good_ref), (spam_cores_ref, spam_ref)):
        count = source.shape[1]
        factor = F32(hosts / count)
        block_iota = lax.broadcasted_iota(jnp.int32, (blocks, count), 0) * size
        lane_iota = lax.broadcasted_iota(jnp.int32, (size, count), 0)

        def one(s, _):
            local = source[pl.ds(s, 1), :] - base
            shifted = local - block_iota
            inside = jnp.where((shifted >= 0) & (shifted < size), F32(1), F32(0)).astype(BF16)
            start = jnp.max(jnp.where(local >= block_iota, block_iota, 0), axis=0, keepdims=True)
            lane = jnp.where(lane_iota == local - start, F32(1), F32(0)).astype(BF16)
            counts = lax.dot_general(
                inside, lane, (((1,), (1,)), ((), ())), preferred_element_type=F32
            )
            for b in range(blocks):
                target[b, pl.ds(s, 1), :] = counts[b : b + 1, :] * factor
            return 0

        lax.fori_loop(0, seeds, one, 0, unroll=4)


def exponent_of(peak):
    return jnp.floor(jnp.log2(jnp.maximum(peak, F32(2.0**-100)))) + F32(1)


def to_words(value):
    return jnp.clip(jnp.floor(value + F32(0.5)), F32(-32767), F32(32767))


def pack(first, cap, acc, out_ref):
    peers = out_ref.shape[0]
    size = acc.shape[2]
    tail = out_ref.shape[1] - cap * size

    def one(p, _):
        exps, cols = [], []
        for c in range(cap):
            n = p * cap + c
            value = acc[n, :size, :]
            e = exponent_of(jnp.max(jnp.abs(value), axis=0, keepdims=True))
            out_ref[p, c * size : (c + 1) * size, :] = to_words(value * jnp.exp2(WORD - e)).astype(
                jnp.int32
            ).astype(jnp.int16)
            exps.append(e)
            if first:
                col = acc[n, size : size + 8, :][:1, :]
                f = exponent_of(jnp.abs(col))
                scaled = col * jnp.exp2(WORD - f)
                high = to_words(scaled)
                cols += [f, high, to_words((scaled - high) * F32(2.0**WORD))]
        rows = exps + cols
        if tail > len(rows):
            rows.append(jnp.zeros((tail - len(rows), size), F32))
        out_ref[p, cap * size :, :] = jnp.concatenate(rows, axis=0).astype(jnp.int32).astype(jnp.int16)
        return 0

    lax.fori_loop(0, peers, one, 0)


def push_kernel(first, cap, *refs):
    if first:
        src_ref, slot_ref, good_ref, degree_ref, tiles_ref, out_ref, acc, scaled = refs
    else:
        src_ref, slot_ref, inflow, good_ref, degree_ref, tiles_ref, out_ref, acc, scaled = refs
    step = pl.program_id(0)
    blocks, seeds, size = good_ref.shape
    per_step = tiles_ref.shape[0]

    @pl.when(step == 0)
    def _():
        acc[...] = jnp.zeros_like(acc)
        def one(b, _):
            degree = degree_ref[b].astype(F32)
            trust = good_ref[b]
            if not first:
                trust = F32(0.85) * inflow[b] + F32(0.15) * trust
            scaled[b, :seeds, :] = (trust / degree).astype(BF16)
            if first:
                scaled[b, seeds:, :] = jnp.ones((scaled.shape[1] - seeds, size), BF16)
            return 0

        lax.fori_loop(0, blocks, one, 0)

    def one(k, _):
        n = step * per_step + k
        acc[slot_ref[n]] += jnp.dot(scaled[src_ref[n]], tiles_ref[k], preferred_element_type=F32)
        return 0

    lax.fori_loop(0, per_step, one, 0, unroll=4)

    @pl.when(step == pl.num_programs(0) - 1)
    def _():
        pack(first, cap, acc, out_ref)


def shares(shield_ref, weight_ref, start_of, share_ref):
    def one(b, _):
        share_ref[b] = (shield_ref[b] * start_of(b) / weight_ref[b]).astype(BF16)
        return 0

    lax.fori_loop(0, share_ref.shape[0], one, 0)


def greet(devices):
    barrier = pltpu.get_barrier_semaphore()
    for device, there in devices:
        @pl.when(there)
        def _():
            pl.semaphore_signal(barrier, inc=1, device_id=device, device_id_type=MESH)
    pl.semaphore_wait(barrier, sum(jnp.where(there, 1, 0) for _, there in devices))


def fetch_kernel(rows, columns, cap, want_ref, share_ref, fetched_ref, *scratch):
    line = 2 * (columns - 1)
    held, (picked, line_send, line_recv, send, recv) = scratch[:line], scratch[line:]
    r, z = lax.axis_index("row"), lax.axis_index("col")
    others = [lax.rem(r + d, rows) for d in range(1, rows)]
    sides = (-1, 1)
    inside = {side: (z + side >= 0) & (z + side < columns) for side in sides}
    greet([((t, z), t >= 0) for t in others] + [((r, z + side), inside[side]) for side in sides])

    def place(side, d):
        return 2 * (d - 1) + (0 if side < 0 else 1)

    def pass_on(source, d, side):
        slot = place(-side, d)
        return pltpu.make_async_remote_copy(
            src_ref=source, dst_ref=held[slot],
            send_sem=line_send.at[slot], recv_sem=line_recv.at[slot],
            device_id=(r, z + side), device_id_type=MESH,
        )

    def serve(t, origin):
        return pltpu.make_async_remote_copy(
            src_ref=picked.at[t, pl.ds(origin * cap, cap)],
            dst_ref=fetched_ref.at[pl.ds((r * columns + origin) * cap, cap)],
            send_sem=send.at[t, origin], recv_sem=recv.at[r, origin],
            device_id=(t, z), device_id_type=MESH,
        )

    def spread(source, origin):
        before = None
        for t in others:
            for j in range(cap):
                picked[t, origin * cap + j] = source[want_ref[t, origin * cap + j]]
            if before is not None:
                serve(before, origin).start()
            before = t
        for j in range(cap):
            fetched_ref[(r * columns + origin) * cap + j] = source[want_ref[r, origin * cap + j]]
        serve(before, origin).start()

    for side in sides:
        @pl.when(inside[side])
        def _():
            pass_on(share_ref, 1, side).start()
    spread(share_ref, z)
    for d in range(1, columns):
        for side in sides:
            origin = z + side * d

            @pl.when((origin >= 0) & (origin < columns))
            def _():
                here = held[place(side, d)]
                pass_on(share_ref, d, -side).wait_recv()

                if d < columns - 1:
                    @pl.when(inside[-side])
                    def _():
                        pass_on(here, d + 1, -side).start()

                spread(here, origin)
    for origin in range(columns):
        for t in others:
            serve(t, origin).wait_send()
            pltpu.make_async_remote_copy(
                src_ref=picked.at[t, pl.ds(origin * cap, cap)],
                dst_ref=fetched_ref.at[pl.ds((t * columns + origin) * cap, cap)],
                send_sem=send.at[t, origin], recv_sem=recv.at[t, origin],
                device_id=(t, z), device_id_type=MESH,
            ).wait_recv()
    for d in range(columns - 1):
        for side in sides:
            origin = z - side * d

            @pl.when((origin >= 0) & (origin < columns) & inside[side])
            def _():
                pass_on(share_ref, d + 1, side).wait_send()


def reduce_kernel(first, rows, columns, cap, want_ref, words_ref, *refs):
    inflow_ref, refs = refs[0], refs[1:]
    if first:
        weight_ref, refs = refs[0], refs[1:]
    (landed, table, partial, exps, scales, packed, final,
     own, send, recv, line_send, line_recv) = refs
    r, z = lax.axis_index("row"), lax.axis_index("col")
    blocks, seeds, size = partial.shape
    others = [lax.rem(r + d, rows) for d in range(1, rows)]
    order = [columns // 2] + [d for d in range(1, columns) if d != columns // 2] + [0]
    block_iota = lax.broadcasted_iota(jnp.int32, (blocks, size), 0)
    data = blocks * seeds
    greet(
        [((t, z), t >= 0) for t in others]
        + [((r, lax.rem(z + d, columns)), z >= 0) for d in range(1, columns)]
    )

    def across(d, t, origin):
        return pltpu.make_async_remote_copy(
            src_ref=words_ref.at[t * columns + lax.rem(z + d, columns)], dst_ref=landed.at[d, origin],
            send_sem=send.at[d, t], recv_sem=recv.at[d, origin], device_id=(t, z), device_id_type=MESH,
        )

    def mine(d):
        return pltpu.make_async_copy(
            words_ref.at[r * columns + lax.rem(z + d, columns)], landed.at[d, r], own.at[d]
        )

    def along(d):
        return pltpu.make_async_remote_copy(
            src_ref=packed.at[d - 1], dst_ref=final.at[d - 1],
            send_sem=line_send.at[d - 1], recv_sem=line_recv.at[d - 1],
            device_id=(r, lax.rem(z + d, columns)), device_id_type=MESH,
        )

    def to_int16(value):
        return value.astype(jnp.int32).astype(jnp.int16)

    def to_float(value):
        return value.astype(jnp.int32).astype(F32)

    for d in order:
        for t in others:
            across(d, t, r).start()
        mine(d).start()

    cols = jnp.zeros((blocks, size), F32)
    for d in order:
        y = lax.rem(z + d, columns)
        mine(d).wait()
        for t in others:
            across(d, t, t).wait_recv()

        def weigh(q, cols):
            tail = to_float(landed[d, q, cap * seeds :, :])
            for c in range(cap):
                hit = block_iota == want_ref[q, y * cap + c]
                scale = jnp.exp2(tail[c : c + 1, :] - WORD)
                table[q * cap + c] = jnp.where(hit, jnp.broadcast_to(scale, (blocks, size)), F32(0))
                if first:
                    f, high, low = (tail[cap + 3 * c + i : cap + 3 * c + i + 1, :] for i in range(3))
                    col = (high + low * F32(2.0**-WORD)) * jnp.exp2(f - WORD)
                    cols = cols + jnp.where(hit, jnp.broadcast_to(col, (blocks, size)), F32(0))
            return cols

        cols = lax.fori_loop(0, rows, weigh, jnp.zeros((blocks, size), F32))

        def strip(i, _):
            at = pl.multiple_of(i * 16, 16)

            def add(q, sums):
                sums = list(sums)
                for c in range(cap):
                    value = to_float(landed[d, q, pl.ds(pl.multiple_of(c * seeds + at, 16), 16), :])
                    for b in range(blocks):
                        sums[b] = sums[b] + value * table[q * cap + c, b : b + 1, :]
                return tuple(sums)

            sums = lax.fori_loop(0, rows, add, (jnp.zeros((16, size), F32),) * blocks)
            for b in range(blocks):
                partial[b, pl.ds(at, 16), :] = sums[b]
            return 0

        lax.fori_loop(0, seeds // 16, strip, 0)
        if d:
            def squeeze(b, _):
                value = partial[b]
                e = exponent_of(jnp.max(jnp.abs(value), axis=0, keepdims=True))
                exps[pl.ds(b, 1), :] = e
                packed[d - 1, pl.ds(pl.multiple_of(b * seeds, seeds), seeds), :] = to_int16(
                    to_words(value * jnp.exp2(WORD - e))
                )
                return 0

            lax.fori_loop(0, blocks, squeeze, 0)
            packed[d - 1, data : data + blocks, :] = to_int16(exps[...])
            if first:
                f = exponent_of(jnp.abs(cols))
                scaled = cols * jnp.exp2(WORD - f)
                high = to_words(scaled)
                for i, row in enumerate((f, high, to_words((scaled - high) * F32(2.0**WORD)))):
                    packed[d - 1, data + (i + 1) * blocks : data + (i + 2) * blocks, :] = to_int16(row)
            along(d).start()

    for d in order[:-1]:
        along(d).wait_recv()
        scales[d - 1] = jnp.exp2(to_float(final[d - 1, data : data + blocks, :]) - WORD)
        if first:
            f, high, low = (
                to_float(final[d - 1, data + (i + 1) * blocks : data + (i + 2) * blocks, :])
                for i in range(3)
            )
            cols = cols + (high + low * F32(2.0**-WORD)) * jnp.exp2(f - WORD)
    if first:
        for b in range(blocks):
            weight_ref[b] = F32(1) + cols[b : b + 1, :]

    def finish(b, _):
        total = partial[b]
        for d in range(1, columns):
            value = to_float(final[d - 1, pl.ds(pl.multiple_of(b * seeds, seeds), seeds), :])
            total = total + value * scales[d - 1, pl.ds(b, 1), :]
        inflow_ref[b] = total
        return 0

    lax.fori_loop(0, blocks, finish, 0)
    for d in order:
        for t in others:
            across(d, t, r).wait_send()
    for d in order[:-1]:
        along(d).wait_send()


def trust_kernel(inflow, good_ref, spam_ref, weight_ref, trust_ref, shield_ref, share_ref):
    size = inflow.shape[2]

    def one(b, _):
        trust = F32(0.85) * inflow[b] + F32(0.15) * good_ref[b]
        trust_ref[pl.ds(pl.multiple_of(b * size, size), size), :] = jnp.transpose(trust)
        shield_ref[b] = F32(1) / (F32(1) + trust)
        return 0

    lax.fori_loop(0, inflow.shape[0], one, 0)
    shares(shield_ref, weight_ref, lambda b: spam_ref[b], share_ref)


def pull_kernel(last, *refs):
    if last:
        src_ref, slot_ref, fetched_ref, spam_ref, tiles_ref, out_ref, acc = refs
    else:
        (src_ref, slot_ref, fetched_ref, spam_ref, shield_ref, weight_ref, tiles_ref,
         out_ref, acc) = refs
    step = pl.program_id(0)
    per_step = tiles_ref.shape[0]
    size = acc.shape[2]

    @pl.when(step == 0)
    def _():
        acc[...] = jnp.zeros_like(acc)

    def one(k, _):
        n = step * per_step + k
        acc[src_ref[n]] += lax.dot_general(
            fetched_ref[slot_ref[n]], tiles_ref[k], (((1,), (1,)), ((), ())),
            preferred_element_type=F32,
        )
        return 0

    lax.fori_loop(0, per_step, one, 0, unroll=4)

    @pl.when(step == pl.num_programs(0) - 1)
    def _():
        def distrust(b):
            return F32(0.85) * acc[b] + F32(0.15) * spam_ref[b]

        if last:
            def one(b, _):
                out_ref[pl.ds(pl.multiple_of(b * size, size), size), :] = jnp.transpose(distrust(b))
                return 0

            lax.fori_loop(0, acc.shape[0], one, 0)
        else:
            shares(shield_ref, weight_ref, distrust, out_ref)


def body(columns, tiles, tile_src, tile_slot, slot_block, out_degree, good_seeds, spam_cores):
    tile_count, size, _ = tiles.shape
    hosts = out_degree.shape[0]
    blocks = hosts // size
    seeds = good_seeds.shape[0]
    slots = slot_block.shape[0]
    peers = lax.axis_size(AXES)
    cap = slots // peers
    tail = -(-4 * cap // 16) * 16
    steps = 8
    shape = jax.ShapeDtypeStruct
    vector = (blocks, seeds, size)
    degree = out_degree.reshape(blocks, 1, size)

    rows = peers // columns
    want = lax.all_to_all(
        slot_block.reshape(rows, columns * cap), "row", split_axis=0, concat_axis=0, tiled=True
    )
    good, spam = pl.pallas_call(
        functools.partial(seed_kernel, columns),
        out_shape=(shape(vector, F32), shape(vector, F32)),
        in_specs=[VM, VM],
        out_specs=(VM, VM),
    )(good_seeds, spam_cores)

    tile_spec = pl.BlockSpec((tile_count // steps, size, size), lambda i: (i, 0, 0))
    words = shape((peers, cap * size + tail, size), jnp.int16)
    outgoing = pl.pallas_call(
        functools.partial(push_kernel, True, cap),
        grid=(steps,),
        out_shape=words,
        in_specs=[SM, SM, VM, VM, tile_spec],
        out_specs=VM,
        scratch_shapes=[
            pltpu.VMEM((slots, seeds + 16, size), F32),
            pltpu.VMEM((blocks, seeds + 16, size), BF16),
        ],
    )(tile_src, tile_slot, good, degree, tiles)
    def reduce(first, words_in):
        long = blocks * seeds + blocks * (4 if first else 1)
        outs = (shape(vector, F32), shape((blocks, 1, size), F32))
        return pl.pallas_call(
            functools.partial(reduce_kernel, first, rows, columns, cap),
            out_shape=outs if first else outs[:1],
            in_specs=[SM, VM],
            out_specs=(VM, VM) if first else (VM,),
            scratch_shapes=[
                pltpu.VMEM((columns, rows, cap * size + tail, size), jnp.int16),
                pltpu.VMEM((rows * cap, blocks, size), F32),
                pltpu.VMEM(vector, F32),
                pltpu.VMEM((blocks, size), F32),
                pltpu.VMEM((columns - 1, blocks, size), F32),
                pltpu.VMEM((columns - 1, long, size), jnp.int16),
                pltpu.VMEM((columns - 1, long, size), jnp.int16),
                pltpu.SemaphoreType.DMA((columns,)),
                pltpu.SemaphoreType.DMA((columns, rows)),
                pltpu.SemaphoreType.DMA((columns, rows)),
                pltpu.SemaphoreType.DMA((columns - 1,)),
                pltpu.SemaphoreType.DMA((columns - 1,)),
            ],
            compiler_params=pltpu.CompilerParams(
                collective_id=1 if first else 2, has_side_effects=True
            ),
        )(want, words_in)

    inflow, weight = reduce(True, outgoing)
    outgoing = pl.pallas_call(
        functools.partial(push_kernel, False, cap),
        grid=(steps,),
        out_shape=words,
        in_specs=[SM, SM, VM, VM, VM, tile_spec],
        out_specs=VM,
        scratch_shapes=[
            pltpu.VMEM((slots, seeds, size), F32),
            pltpu.VMEM(vector, BF16),
        ],
    )(tile_src, tile_slot, inflow, good, degree, tiles)
    (inflow,) = reduce(False, outgoing)
    fetch = pl.pallas_call(
        functools.partial(fetch_kernel, rows, columns, cap),
        out_shape=shape((slots, seeds, size), BF16),
        in_specs=[SM, VM],
        out_specs=VM,
        scratch_shapes=[
            *[pltpu.VMEM(vector, BF16)] * (2 * columns - 2),
            pltpu.VMEM((rows, columns * cap, seeds, size), BF16),
            pltpu.SemaphoreType.DMA((2 * columns - 2,)),
            pltpu.SemaphoreType.DMA((2 * columns - 2,)),
            pltpu.SemaphoreType.DMA((rows, columns)),
            pltpu.SemaphoreType.DMA((rows, columns)),
        ],
        compiler_params=pltpu.CompilerParams(collective_id=0, has_side_effects=True),
    )
    trust, shield, share = pl.pallas_call(
        trust_kernel,
        out_shape=(shape((hosts, seeds), F32), shape(vector, F32), shape(vector, BF16)),
        in_specs=[VM, VM, VM, VM],
        out_specs=(VM, VM, VM),
    )(inflow, good, spam, weight)
    fetched = fetch(want, share)
    share = pl.pallas_call(
        functools.partial(pull_kernel, False),
        grid=(steps,),
        out_shape=shape(vector, BF16),
        in_specs=[SM, SM, VM, VM, VM, VM, tile_spec],
        out_specs=VM,
        scratch_shapes=[pltpu.VMEM(vector, F32)],
    )(tile_src, tile_slot, fetched, spam, shield, weight, tiles)
    fetched = fetch(want, share)
    distrust = pl.pallas_call(
        functools.partial(pull_kernel, True),
        grid=(steps,),
        out_shape=shape((hosts, seeds), F32),
        in_specs=[SM, SM, VM, VM, tile_spec],
        out_specs=VM,
        scratch_shapes=[pltpu.VMEM(vector, F32)],
    )(tile_src, tile_slot, fetched, spam, tiles)
    return trust, distrust


def solution(mesh):
    in_specs = (
        P(AXES, None, None),
        P(AXES),
        P(AXES),
        P(AXES),
        P(AXES),
        P(None, AXES),
        P(None, AXES),
    )
    out_specs = (P(AXES, None), P(AXES, None))
    return jax.shard_map(
        functools.partial(body, mesh.shape["col"]),
        mesh=mesh, in_specs=in_specs, out_specs=out_specs, check_vma=False,
    )
```

```python
import functools

import jax
import jax.numpy as jnp
from jax import lax
from jax.experimental import pallas as pl
from jax.experimental.pallas import tpu as pltpu
from jax.sharding import PartitionSpec as P

AXES = ("row", "col")
VM = pl.BlockSpec(memory_space=pltpu.VMEM)
SM = pl.BlockSpec(memory_space=pltpu.SMEM)
F32 = jnp.float32
BF16 = jnp.bfloat16
WORD = 15
GROUP = 4
MESH = pl.DeviceIdType.MESH


def count_seeds(columns, source, target):
    blocks, seeds, size = target.shape
    hosts = blocks * size
    base = (lax.axis_index("row") * columns + lax.axis_index("col")) * hosts
    count = source.shape[1]
    factor = F32(hosts / count)
    block_iota = lax.broadcasted_iota(jnp.int32, (blocks, count), 0) * size
    lane_iota = lax.broadcasted_iota(jnp.int32, (size, count), 0)

    def one(s, _):
        local = source[pl.ds(s, 1), :] - base
        shifted = local - block_iota
        inside = jnp.where((shifted >= 0) & (shifted < size), F32(1), F32(0)).astype(BF16)
        start = jnp.max(jnp.where(local >= block_iota, block_iota, 0), axis=0, keepdims=True)
        lane = jnp.where(lane_iota == local - start, F32(1), F32(0)).astype(BF16)
        counts = lax.dot_general(
            inside, lane, (((1,), (1,)), ((), ())), preferred_element_type=F32
        )
        for b in range(blocks):
            target[b, pl.ds(s, 1), :] = counts[b : b + 1, :] * factor
        return 0

    lax.fori_loop(0, seeds, one, 0, unroll=4)


def exponent_of(peak):
    return jnp.floor(jnp.log2(jnp.maximum(peak, F32(2.0**-100)))) + F32(1)


def to_words(value):
    return jnp.clip(jnp.floor(value + F32(0.5)), F32(-32767), F32(32767))


def pack(first, cap, acc, out_ref):
    peers = out_ref.shape[0]
    size = acc.shape[2]
    tail = out_ref.shape[1] - cap * size

    def one(p, _):
        exps, cols = [], []
        for c in range(cap):
            n = p * cap + c
            value = acc[n, :size, :]
            e = exponent_of(jnp.max(jnp.abs(value), axis=0, keepdims=True))
            out_ref[p, c * size : (c + 1) * size, :] = to_words(value * jnp.exp2(WORD - e)).astype(
                jnp.int32
            ).astype(jnp.int16)
            exps.append(e)
            if first:
                col = acc[n, size : size + 8, :][:1, :]
                f = exponent_of(jnp.abs(col))
                scaled = col * jnp.exp2(WORD - f)
                high = to_words(scaled)
                cols += [f, high, to_words((scaled - high) * F32(2.0**WORD))]
        rows = exps + cols
        if tail > len(rows):
            rows.append(jnp.zeros((tail - len(rows), size), F32))
        out_ref[p, cap * size :, :] = jnp.concatenate(rows, axis=0).astype(jnp.int32).astype(jnp.int16)
        return 0

    lax.fori_loop(0, peers, one, 0)


def push_kernel(first, cap, *refs):
    if first:
        src_ref, slot_ref, good_ref, degree_ref, tiles_ref, out_ref, acc, scaled = refs
    else:
        src_ref, slot_ref, inflow, good_ref, degree_ref, tiles_ref, out_ref, acc, scaled = refs
    step = pl.program_id(0)
    blocks, seeds, size = good_ref.shape
    per_step = tiles_ref.shape[0]

    @pl.when(step == 0)
    def _():
        acc[...] = jnp.zeros_like(acc)
        def one(b, _):
            degree = degree_ref[b].astype(F32)
            trust = good_ref[b]
            if not first:
                trust = F32(0.85) * inflow[b] + F32(0.15) * trust
            scaled[b, :seeds, :] = (trust / degree).astype(BF16)
            if first:
                scaled[b, seeds:, :] = jnp.ones((scaled.shape[1] - seeds, size), BF16)
            return 0

        lax.fori_loop(0, blocks, one, 0)

    def some(g, _):
        products = []
        for k in range(GROUP):
            n = step * per_step + g * GROUP + k
            products.append(
                jnp.dot(scaled[src_ref[n]], tiles_ref[g * GROUP + k], preferred_element_type=F32)
            )
        for k in range(GROUP):
            acc[slot_ref[step * per_step + g * GROUP + k]] += products[k]
        return 0

    lax.fori_loop(0, per_step // GROUP, some, 0)

    @pl.when(step == pl.num_programs(0) - 1)
    def _():
        pack(first, cap, acc, out_ref)


def shares(shield_ref, weight_ref, start_of, share_ref):
    def one(b, _):
        share_ref[b] = (shield_ref[b] * start_of(b) / weight_ref[b]).astype(BF16)
        return 0

    lax.fori_loop(0, share_ref.shape[0], one, 0)


def greet(devices):
    barrier = pltpu.get_barrier_semaphore()
    for device, there in devices:
        @pl.when(there)
        def _():
            pl.semaphore_signal(barrier, inc=1, device_id=device, device_id_type=MESH)
    pl.semaphore_wait(barrier, sum(jnp.where(there, 1, 0) for _, there in devices))


def fetch_kernel(rows, columns, cap, want_ref, share_ref, fetched_ref, *scratch):
    line = 2 * (columns - 1)
    held, (picked, line_send, line_recv, send, recv) = scratch[:line], scratch[line:]
    r, z = lax.axis_index("row"), lax.axis_index("col")
    others = [lax.rem(r + d, rows) for d in range(1, rows)]
    sides = (-1, 1)
    inside = {side: (z + side >= 0) & (z + side < columns) for side in sides}
    greet([((t, z), t >= 0) for t in others] + [((r, z + side), inside[side]) for side in sides])

    def place(side, d):
        return 2 * (d - 1) + (0 if side < 0 else 1)

    def pass_on(source, d, side):
        slot = place(-side, d)
        return pltpu.make_async_remote_copy(
            src_ref=source, dst_ref=held[slot],
            send_sem=line_send.at[slot], recv_sem=line_recv.at[slot],
            device_id=(r, z + side), device_id_type=MESH,
        )

    def serve(t, origin):
        return pltpu.make_async_remote_copy(
            src_ref=picked.at[t, pl.ds(origin * cap, cap)],
            dst_ref=fetched_ref.at[pl.ds((r * columns + origin) * cap, cap)],
            send_sem=send.at[t, origin], recv_sem=recv.at[r, origin],
            device_id=(t, z), device_id_type=MESH,
        )

    def spread(source, origin):
        before = None
        for t in others:
            for j in range(cap):
                picked[t, origin * cap + j] = source[want_ref[t, origin * cap + j]]
            if before is not None:
                serve(before, origin).start()
            before = t
        for j in range(cap):
            fetched_ref[(r * columns + origin) * cap + j] = source[want_ref[r, origin * cap + j]]
        serve(before, origin).start()

    for side in sides:
        @pl.when(inside[side])
        def _():
            pass_on(share_ref, 1, side).start()
    spread(share_ref, z)
    for d in range(1, columns):
        for side in sides:
            origin = z + side * d

            @pl.when((origin >= 0) & (origin < columns))
            def _():
                here = held[place(side, d)]
                pass_on(share_ref, d, -side).wait_recv()

                if d < columns - 1:
                    @pl.when(inside[-side])
                    def _():
                        pass_on(here, d + 1, -side).start()

                spread(here, origin)
    for origin in range(columns):
        for t in others:
            serve(t, origin).wait_send()
            pltpu.make_async_remote_copy(
                src_ref=picked.at[t, pl.ds(origin * cap, cap)],
                dst_ref=fetched_ref.at[pl.ds((t * columns + origin) * cap, cap)],
                send_sem=send.at[t, origin], recv_sem=recv.at[t, origin],
                device_id=(t, z), device_id_type=MESH,
            ).wait_recv()
    for d in range(columns - 1):
        for side in sides:
            origin = z - side * d

            @pl.when((origin >= 0) & (origin < columns) & inside[side])
            def _():
                pass_on(share_ref, d + 1, side).wait_send()


def reduce_kernel(first, rows, columns, cap, want_ref, words_ref, *refs):
    if first:
        cores_ref, inflow_ref, weight_ref, spam_ref, *refs = refs
    else:
        inflow_ref, *refs = refs
    (landed, table, partial, exps, scales, packed, final,
     own, send, recv, line_send, line_recv) = refs
    r, z = lax.axis_index("row"), lax.axis_index("col")
    blocks, seeds, size = partial.shape
    others = [lax.rem(r + d, rows) for d in range(1, rows)]
    order = [columns // 2] + [d for d in range(1, columns) if d != columns // 2] + [0]
    block_iota = lax.broadcasted_iota(jnp.int32, (blocks, size), 0)
    data = blocks * seeds
    greet(
        [((t, z), t >= 0) for t in others]
        + [((r, lax.rem(z + d, columns)), z >= 0) for d in range(1, columns)]
    )

    def across(d, t, origin):
        return pltpu.make_async_remote_copy(
            src_ref=words_ref.at[t * columns + lax.rem(z + d, columns)], dst_ref=landed.at[d, origin],
            send_sem=send.at[d, t], recv_sem=recv.at[d, origin], device_id=(t, z), device_id_type=MESH,
        )

    def mine(d):
        return pltpu.make_async_copy(
            words_ref.at[r * columns + lax.rem(z + d, columns)], landed.at[d, r], own.at[d]
        )

    def along(d):
        return pltpu.make_async_remote_copy(
            src_ref=packed.at[d - 1], dst_ref=final.at[d - 1],
            send_sem=line_send.at[d - 1], recv_sem=line_recv.at[d - 1],
            device_id=(r, lax.rem(z + d, columns)), device_id_type=MESH,
        )

    def to_int16(value):
        return value.astype(jnp.int32).astype(jnp.int16)

    def to_float(value):
        return value.astype(jnp.int32).astype(F32)

    for d in order:
        for t in others:
            across(d, t, r).start()
        mine(d).start()
    if first:
        count_seeds(columns, cores_ref, spam_ref)

    cols = jnp.zeros((blocks, size), F32)
    for d in order:
        y = lax.rem(z + d, columns)
        mine(d).wait()
        for t in others:
            across(d, t, t).wait_recv()

        def weigh(q, cols):
            tail = to_float(landed[d, q, cap * seeds :, :])
            for c in range(cap):
                hit = block_iota == want_ref[q, y * cap + c]
                scale = jnp.exp2(tail[c : c + 1, :] - WORD)
                table[q * cap + c] = jnp.where(hit, jnp.broadcast_to(scale, (blocks, size)), F32(0))
                if first:
                    f, high, low = (tail[cap + 3 * c + i : cap + 3 * c + i + 1, :] for i in range(3))
                    col = (high + low * F32(2.0**-WORD)) * jnp.exp2(f - WORD)
                    cols = cols + jnp.where(hit, jnp.broadcast_to(col, (blocks, size)), F32(0))
            return cols

        cols = lax.fori_loop(0, rows, weigh, jnp.zeros((blocks, size), F32))

        def strip(i, _):
            at = pl.multiple_of(i * 16, 16)

            def add(q, sums):
                sums = list(sums)
                for c in range(cap):
                    value = to_float(landed[d, q, pl.ds(pl.multiple_of(c * seeds + at, 16), 16), :])
                    for b in range(blocks):
                        sums[b] = sums[b] + value * table[q * cap + c, b : b + 1, :]
                return tuple(sums)

            sums = lax.fori_loop(0, rows, add, (jnp.zeros((16, size), F32),) * blocks)
            for b in range(blocks):
                partial[b, pl.ds(at, 16), :] = sums[b]
            return 0

        lax.fori_loop(0, seeds // 16, strip, 0)
        if d:
            def squeeze(b, _):
                value = partial[b]
                e = exponent_of(jnp.max(jnp.abs(value), axis=0, keepdims=True))
                exps[pl.ds(b, 1), :] = e
                packed[d - 1, pl.ds(pl.multiple_of(b * seeds, seeds), seeds), :] = to_int16(
                    to_words(value * jnp.exp2(WORD - e))
                )
                return 0

            lax.fori_loop(0, blocks, squeeze, 0)
            packed[d - 1, data : data + blocks, :] = to_int16(exps[...])
            if first:
                f = exponent_of(jnp.abs(cols))
                scaled = cols * jnp.exp2(WORD - f)
                high = to_words(scaled)
                for i, row in enumerate((f, high, to_words((scaled - high) * F32(2.0**WORD)))):
                    packed[d - 1, data + (i + 1) * blocks : data + (i + 2) * blocks, :] = to_int16(row)
            along(d).start()

    for d in order[:-1]:
        along(d).wait_recv()
        scales[d - 1] = jnp.exp2(to_float(final[d - 1, data : data + blocks, :]) - WORD)
        if first:
            f, high, low = (
                to_float(final[d - 1, data + (i + 1) * blocks : data + (i + 2) * blocks, :])
                for i in range(3)
            )
            cols = cols + (high + low * F32(2.0**-WORD)) * jnp.exp2(f - WORD)
    if first:
        for b in range(blocks):
            weight_ref[b] = F32(1) + cols[b : b + 1, :]

    def finish(b, _):
        total = partial[b]
        for d in range(1, columns):
            value = to_float(final[d - 1, pl.ds(pl.multiple_of(b * seeds, seeds), seeds), :])
            total = total + value * scales[d - 1, pl.ds(b, 1), :]
        inflow_ref[b] = total
        return 0

    lax.fori_loop(0, blocks, finish, 0)
    for d in order:
        for t in others:
            across(d, t, r).wait_send()
    for d in order[:-1]:
        along(d).wait_send()


def trust_kernel(inflow, good_ref, spam_ref, weight_ref, trust_ref, shield_ref, share_ref):
    size = inflow.shape[2]

    def one(b, _):
        trust = F32(0.85) * inflow[b] + F32(0.15) * good_ref[b]
        trust_ref[pl.ds(pl.multiple_of(b * size, size), size), :] = jnp.transpose(trust)
        shield_ref[b] = F32(1) / (F32(1) + trust)
        return 0

    lax.fori_loop(0, inflow.shape[0], one, 0)
    shares(shield_ref, weight_ref, lambda b: spam_ref[b], share_ref)


def pull_kernel(last, *refs):
    if last:
        src_ref, slot_ref, fetched_ref, spam_ref, tiles_ref, out_ref, acc = refs
    else:
        (src_ref, slot_ref, fetched_ref, spam_ref, shield_ref, weight_ref, tiles_ref,
         out_ref, acc) = refs
    step = pl.program_id(0)
    per_step = tiles_ref.shape[0]
    size = acc.shape[2]

    @pl.when(step == 0)
    def _():
        acc[...] = jnp.zeros_like(acc)

    def some(g, _):
        products = []
        for k in range(GROUP):
            n = step * per_step + g * GROUP + k
            products.append(
                lax.dot_general(
                    fetched_ref[slot_ref[n]], tiles_ref[g * GROUP + k], (((1,), (1,)), ((), ())),
                    preferred_element_type=F32,
                )
            )
        for k in range(GROUP):
            acc[src_ref[step * per_step + g * GROUP + k]] += products[k]
        return 0

    lax.fori_loop(0, per_step // GROUP, some, 0)

    @pl.when(step == pl.num_programs(0) - 1)
    def _():
        def distrust(b):
            return F32(0.85) * acc[b] + F32(0.15) * spam_ref[b]

        if last:
            def one(b, _):
                out_ref[pl.ds(pl.multiple_of(b * size, size), size), :] = jnp.transpose(distrust(b))
                return 0

            lax.fori_loop(0, acc.shape[0], one, 0)
        else:
            shares(shield_ref, weight_ref, distrust, out_ref)


def body(columns, tiles, tile_src, tile_slot, slot_block, out_degree, good_seeds, spam_cores):
    tile_count, size, _ = tiles.shape
    hosts = out_degree.shape[0]
    blocks = hosts // size
    seeds = good_seeds.shape[0]
    slots = slot_block.shape[0]
    peers = lax.axis_size(AXES)
    cap = slots // peers
    tail = -(-4 * cap // 16) * 16
    steps = 8
    shape = jax.ShapeDtypeStruct
    vector = (blocks, seeds, size)
    degree = out_degree.reshape(blocks, 1, size)

    rows = peers // columns
    want = lax.all_to_all(
        slot_block.reshape(rows, columns * cap), "row", split_axis=0, concat_axis=0, tiled=True
    )
    good = pl.pallas_call(
        functools.partial(count_seeds, columns),
        out_shape=shape(vector, F32),
        in_specs=[VM],
        out_specs=VM,
    )(good_seeds)

    tile_spec = pl.BlockSpec((tile_count // steps, size, size), lambda i: (i, 0, 0))
    words = shape((peers, cap * size + tail, size), jnp.int16)
    outgoing = pl.pallas_call(
        functools.partial(push_kernel, True, cap),
        grid=(steps,),
        out_shape=words,
        in_specs=[SM, SM, VM, VM, tile_spec],
        out_specs=VM,
        scratch_shapes=[
            pltpu.VMEM((slots, seeds + 16, size), F32),
            pltpu.VMEM((blocks, seeds + 16, size), BF16),
        ],
    )(tile_src, tile_slot, good, degree, tiles)
    def reduce(first, words_in, *rest):
        long = blocks * seeds + blocks * (4 if first else 1)
        outs = (shape(vector, F32), shape((blocks, 1, size), F32), shape(vector, F32))
        return pl.pallas_call(
            functools.partial(reduce_kernel, first, rows, columns, cap),
            out_shape=outs if first else outs[:1],
            in_specs=[SM, VM, VM] if first else [SM, VM],
            out_specs=(VM, VM, VM) if first else (VM,),
            scratch_shapes=[
                pltpu.VMEM((columns, rows, cap * size + tail, size), jnp.int16),
                pltpu.VMEM((rows * cap, blocks, size), F32),
                pltpu.VMEM(vector, F32),
                pltpu.VMEM((blocks, size), F32),
                pltpu.VMEM((columns - 1, blocks, size), F32),
                pltpu.VMEM((columns - 1, long, size), jnp.int16),
                pltpu.VMEM((columns - 1, long, size), jnp.int16),
                pltpu.SemaphoreType.DMA((columns,)),
                pltpu.SemaphoreType.DMA((columns, rows)),
                pltpu.SemaphoreType.DMA((columns, rows)),
                pltpu.SemaphoreType.DMA((columns - 1,)),
                pltpu.SemaphoreType.DMA((columns - 1,)),
            ],
            compiler_params=pltpu.CompilerParams(
                collective_id=1 if first else 2, has_side_effects=True
            ),
        )(want, words_in, *rest)

    inflow, weight, spam = reduce(True, outgoing, spam_cores)
    outgoing = pl.pallas_call(
        functools.partial(push_kernel, False, cap),
        grid=(steps,),
        out_shape=words,
        in_specs=[SM, SM, VM, VM, VM, tile_spec],
        out_specs=VM,
        scratch_shapes=[
            pltpu.VMEM((slots, seeds, size), F32),
            pltpu.VMEM(vector, BF16),
        ],
    )(tile_src, tile_slot, inflow, good, degree, tiles)
    (inflow,) = reduce(False, outgoing)
    fetch = pl.pallas_call(
        functools.partial(fetch_kernel, rows, columns, cap),
        out_shape=shape((slots, seeds, size), BF16),
        in_specs=[SM, VM],
        out_specs=VM,
        scratch_shapes=[
            *[pltpu.VMEM(vector, BF16)] * (2 * columns - 2),
            pltpu.VMEM((rows, columns * cap, seeds, size), BF16),
            pltpu.SemaphoreType.DMA((2 * columns - 2,)),
            pltpu.SemaphoreType.DMA((2 * columns - 2,)),
            pltpu.SemaphoreType.DMA((rows, columns)),
            pltpu.SemaphoreType.DMA((rows, columns)),
        ],
        compiler_params=pltpu.CompilerParams(collective_id=0, has_side_effects=True),
    )
    trust, shield, share = pl.pallas_call(
        trust_kernel,
        out_shape=(shape((hosts, seeds), F32), shape(vector, F32), shape(vector, BF16)),
        in_specs=[VM, VM, VM, VM],
        out_specs=(VM, VM, VM),
    )(inflow, good, spam, weight)
    fetched = fetch(want, share)
    share = pl.pallas_call(
        functools.partial(pull_kernel, False),
        grid=(steps,),
        out_shape=shape(vector, BF16),
        in_specs=[SM, SM, VM, VM, VM, VM, tile_spec],
        out_specs=VM,
        scratch_shapes=[pltpu.VMEM(vector, F32)],
    )(tile_src, tile_slot, fetched, spam, shield, weight, tiles)
    fetched = fetch(want, share)
    distrust = pl.pallas_call(
        functools.partial(pull_kernel, True),
        grid=(steps,),
        out_shape=shape((hosts, seeds), F32),
        in_specs=[SM, SM, VM, VM, tile_spec],
        out_specs=VM,
        scratch_shapes=[pltpu.VMEM(vector, F32)],
    )(tile_src, tile_slot, fetched, spam, tiles)
    return trust, distrust


def solution(mesh):
    in_specs = (
        P(AXES, None, None),
        P(AXES),
        P(AXES),
        P(AXES),
        P(AXES),
        P(None, AXES),
        P(None, AXES),
    )
    out_specs = (P(AXES, None), P(AXES, None))
    return jax.shard_map(
        functools.partial(body, mesh.shape["col"]),
        mesh=mesh, in_specs=in_specs, out_specs=out_specs, check_vma=False,
    )
```

```python
import functools

import jax
import jax.numpy as jnp
from jax import lax
from jax.experimental import pallas as pl
from jax.experimental.pallas import tpu as pltpu
from jax.sharding import PartitionSpec as P

AXES = ("row", "col")
VM = pl.BlockSpec(memory_space=pltpu.VMEM)
SM = pl.BlockSpec(memory_space=pltpu.SMEM)
F32 = jnp.float32
BF16 = jnp.bfloat16
WORD = 15
GROUP = 16
MESH = pl.DeviceIdType.MESH


def count_seeds(columns, source, target):
    blocks, seeds, size = target.shape
    hosts = blocks * size
    base = (lax.axis_index("row") * columns + lax.axis_index("col")) * hosts
    count = source.shape[1]
    factor = F32(hosts / count)
    block_iota = lax.broadcasted_iota(jnp.int32, (blocks, count), 0) * size
    lane_iota = lax.broadcasted_iota(jnp.int32, (size, count), 0)

    def one(s, _):
        local = source[pl.ds(s, 1), :] - base
        shifted = local - block_iota
        inside = jnp.where((shifted >= 0) & (shifted < size), F32(1), F32(0)).astype(BF16)
        start = jnp.max(jnp.where(local >= block_iota, block_iota, 0), axis=0, keepdims=True)
        lane = jnp.where(lane_iota == local - start, F32(1), F32(0)).astype(BF16)
        counts = lax.dot_general(
            inside, lane, (((1,), (1,)), ((), ())), preferred_element_type=F32
        )
        for b in range(blocks):
            target[b, pl.ds(s, 1), :] = counts[b : b + 1, :] * factor
        return 0

    lax.fori_loop(0, seeds, one, 0, unroll=4)


def exponent_of(peak):
    return jnp.floor(jnp.log2(jnp.maximum(peak, F32(2.0**-100)))) + F32(1)


def to_words(value):
    return jnp.clip(jnp.floor(value + F32(0.5)), F32(-32767), F32(32767))


def pack(first, cap, acc, out_ref):
    peers = out_ref.shape[0]
    size = acc.shape[2]
    tail = out_ref.shape[1] - cap * size

    def one(p, _):
        exps, cols = [], []
        for c in range(cap):
            n = p * cap + c
            value = acc[n, :size, :]
            e = exponent_of(jnp.max(jnp.abs(value), axis=0, keepdims=True))
            out_ref[p, c * size : (c + 1) * size, :] = to_words(value * jnp.exp2(WORD - e)).astype(
                jnp.int32
            ).astype(jnp.int16)
            exps.append(e)
            if first:
                col = acc[n, size : size + 8, :][:1, :]
                f = exponent_of(jnp.abs(col))
                scaled = col * jnp.exp2(WORD - f)
                high = to_words(scaled)
                cols += [f, high, to_words((scaled - high) * F32(2.0**WORD))]
        rows = exps + cols
        if tail > len(rows):
            rows.append(jnp.zeros((tail - len(rows), size), F32))
        out_ref[p, cap * size :, :] = jnp.concatenate(rows, axis=0).astype(jnp.int32).astype(jnp.int16)
        return 0

    lax.fori_loop(0, peers, one, 0)


def push_kernel(first, cap, *refs):
    if first:
        src_ref, slot_ref, good_ref, degree_ref, tiles_ref, out_ref, acc, scaled = refs
    else:
        src_ref, slot_ref, inflow, good_ref, degree_ref, tiles_ref, out_ref, acc, scaled = refs
    step = pl.program_id(0)
    blocks, seeds, size = good_ref.shape
    per_step = tiles_ref.shape[0]

    @pl.when(step == 0)
    def _():
        acc[...] = jnp.zeros_like(acc)
        def one(b, _):
            degree = degree_ref[b].astype(F32)
            trust = good_ref[b]
            if not first:
                trust = F32(0.85) * inflow[b] + F32(0.15) * trust
            scaled[b, :seeds, :] = (trust / degree).astype(BF16)
            if first:
                scaled[b, seeds:, :] = jnp.ones((scaled.shape[1] - seeds, size), BF16)
            return 0

        lax.fori_loop(0, blocks, one, 0)

    def some(g, _):
        products = []
        for k in range(GROUP):
            n = step * per_step + g * GROUP + k
            products.append(
                jnp.dot(scaled[src_ref[n]], tiles_ref[g * GROUP + k], preferred_element_type=F32)
            )
        for k in range(GROUP):
            acc[slot_ref[step * per_step + g * GROUP + k]] += products[k]
        return 0

    lax.fori_loop(0, per_step // GROUP, some, 0)

    @pl.when(step == pl.num_programs(0) - 1)
    def _():
        pack(first, cap, acc, out_ref)


def shares(shield_ref, weight_ref, start_of, share_ref):
    def one(b, _):
        share_ref[b] = (shield_ref[b] * start_of(b) / weight_ref[b]).astype(BF16)
        return 0

    lax.fori_loop(0, share_ref.shape[0], one, 0)


def greet(devices):
    barrier = pltpu.get_barrier_semaphore()
    for device, there in devices:
        @pl.when(there)
        def _():
            pl.semaphore_signal(barrier, inc=1, device_id=device, device_id_type=MESH)
    pl.semaphore_wait(barrier, sum(jnp.where(there, 1, 0) for _, there in devices))


def fetch_kernel(rows, columns, cap, want_ref, share_ref, fetched_ref, *scratch):
    line = 2 * (columns - 1)
    held, (picked, line_send, line_recv, send, recv) = scratch[:line], scratch[line:]
    r, z = lax.axis_index("row"), lax.axis_index("col")
    others = [lax.rem(r + d, rows) for d in range(1, rows)]
    sides = (-1, 1)
    inside = {side: (z + side >= 0) & (z + side < columns) for side in sides}
    greet([((t, z), t >= 0) for t in others] + [((r, z + side), inside[side]) for side in sides])

    def place(side, d):
        return 2 * (d - 1) + (0 if side < 0 else 1)

    def pass_on(source, d, side):
        slot = place(-side, d)
        return pltpu.make_async_remote_copy(
            src_ref=source, dst_ref=held[slot],
            send_sem=line_send.at[slot], recv_sem=line_recv.at[slot],
            device_id=(r, z + side), device_id_type=MESH,
        )

    def serve(t, origin):
        return pltpu.make_async_remote_copy(
            src_ref=picked.at[t, pl.ds(origin * cap, cap)],
            dst_ref=fetched_ref.at[pl.ds((r * columns + origin) * cap, cap)],
            send_sem=send.at[t, origin], recv_sem=recv.at[r, origin],
            device_id=(t, z), device_id_type=MESH,
        )

    def spread(source, origin):
        before = None
        for t in others:
            for j in range(cap):
                picked[t, origin * cap + j] = source[want_ref[t, origin * cap + j]]
            if before is not None:
                serve(before, origin).start()
            before = t
        for j in range(cap):
            fetched_ref[(r * columns + origin) * cap + j] = source[want_ref[r, origin * cap + j]]
        serve(before, origin).start()

    for side in sides:
        @pl.when(inside[side])
        def _():
            pass_on(share_ref, 1, side).start()
    spread(share_ref, z)
    for d in range(1, columns):
        for side in sides:
            origin = z + side * d

            @pl.when((origin >= 0) & (origin < columns))
            def _():
                here = held[place(side, d)]
                pass_on(share_ref, d, -side).wait_recv()

                if d < columns - 1:
                    @pl.when(inside[-side])
                    def _():
                        pass_on(here, d + 1, -side).start()

                spread(here, origin)
    for origin in range(columns):
        for t in others:
            serve(t, origin).wait_send()
            pltpu.make_async_remote_copy(
                src_ref=picked.at[t, pl.ds(origin * cap, cap)],
                dst_ref=fetched_ref.at[pl.ds((t * columns + origin) * cap, cap)],
                send_sem=send.at[t, origin], recv_sem=recv.at[t, origin],
                device_id=(t, z), device_id_type=MESH,
            ).wait_recv()
    for d in range(columns - 1):
        for side in sides:
            origin = z - side * d

            @pl.when((origin >= 0) & (origin < columns) & inside[side])
            def _():
                pass_on(share_ref, d + 1, side).wait_send()


def reduce_kernel(first, rows, columns, cap, want_ref, words_ref, *refs):
    if first:
        cores_ref, inflow_ref, weight_ref, spam_ref, *refs = refs
    else:
        inflow_ref, *refs = refs
    (landed, table, partial, exps, scales, packed, final,
     own, send, recv, line_send, line_recv) = refs
    r, z = lax.axis_index("row"), lax.axis_index("col")
    blocks, seeds, size = partial.shape
    others = [lax.rem(r + d, rows) for d in range(1, rows)]
    order = [columns // 2] + [d for d in range(1, columns) if d != columns // 2] + [0]
    block_iota = lax.broadcasted_iota(jnp.int32, (blocks, size), 0)
    data = blocks * seeds
    greet(
        [((t, z), t >= 0) for t in others]
        + [((r, lax.rem(z + d, columns)), z >= 0) for d in range(1, columns)]
    )

    def across(d, t, origin):
        return pltpu.make_async_remote_copy(
            src_ref=words_ref.at[t * columns + lax.rem(z + d, columns)], dst_ref=landed.at[d, origin],
            send_sem=send.at[d, t], recv_sem=recv.at[d, origin], device_id=(t, z), device_id_type=MESH,
        )

    def mine(d):
        return pltpu.make_async_copy(
            words_ref.at[r * columns + lax.rem(z + d, columns)], landed.at[d, r], own.at[d]
        )

    def along(d):
        return pltpu.make_async_remote_copy(
            src_ref=packed.at[d - 1], dst_ref=final.at[d - 1],
            send_sem=line_send.at[d - 1], recv_sem=line_recv.at[d - 1],
            device_id=(r, lax.rem(z + d, columns)), device_id_type=MESH,
        )

    def to_int16(value):
        return value.astype(jnp.int32).astype(jnp.int16)

    def to_float(value):
        return value.astype(jnp.int32).astype(F32)

    for d in order:
        for t in others:
            across(d, t, r).start()
        mine(d).start()
    if first:
        count_seeds(columns, cores_ref, spam_ref)

    cols = jnp.zeros((blocks, size), F32)
    for d in order:
        y = lax.rem(z + d, columns)
        mine(d).wait()
        for t in others:
            across(d, t, t).wait_recv()

        def weigh(q, cols):
            tail = to_float(landed[d, q, cap * seeds :, :])
            for c in range(cap):
                hit = block_iota == want_ref[q, y * cap + c]
                scale = jnp.exp2(tail[c : c + 1, :] - WORD)
                table[q * cap + c] = jnp.where(hit, jnp.broadcast_to(scale, (blocks, size)), F32(0))
                if first:
                    f, high, low = (tail[cap + 3 * c + i : cap + 3 * c + i + 1, :] for i in range(3))
                    col = (high + low * F32(2.0**-WORD)) * jnp.exp2(f - WORD)
                    cols = cols + jnp.where(hit, jnp.broadcast_to(col, (blocks, size)), F32(0))
            return cols

        cols = lax.fori_loop(0, rows, weigh, jnp.zeros((blocks, size), F32))

        def strip(i, _):
            at = pl.multiple_of(i * 16, 16)

            def add(q, sums):
                sums = list(sums)
                for c in range(cap):
                    value = to_float(landed[d, q, pl.ds(pl.multiple_of(c * seeds + at, 16), 16), :])
                    for b in range(blocks):
                        sums[b] = sums[b] + value * table[q * cap + c, b : b + 1, :]
                return tuple(sums)

            sums = lax.fori_loop(0, rows, add, (jnp.zeros((16, size), F32),) * blocks)
            for b in range(blocks):
                partial[b, pl.ds(at, 16), :] = sums[b]
            return 0

        lax.fori_loop(0, seeds // 16, strip, 0)
        if d:
            def squeeze(b, _):
                value = partial[b]
                e = exponent_of(jnp.max(jnp.abs(value), axis=0, keepdims=True))
                exps[pl.ds(b, 1), :] = e
                packed[d - 1, pl.ds(pl.multiple_of(b * seeds, seeds), seeds), :] = to_int16(
                    to_words(value * jnp.exp2(WORD - e))
                )
                return 0

            lax.fori_loop(0, blocks, squeeze, 0)
            packed[d - 1, data : data + blocks, :] = to_int16(exps[...])
            if first:
                f = exponent_of(jnp.abs(cols))
                scaled = cols * jnp.exp2(WORD - f)
                high = to_words(scaled)
                for i, row in enumerate((f, high, to_words((scaled - high) * F32(2.0**WORD)))):
                    packed[d - 1, data + (i + 1) * blocks : data + (i + 2) * blocks, :] = to_int16(row)
            along(d).start()

    for d in order[:-1]:
        along(d).wait_recv()
        scales[d - 1] = jnp.exp2(to_float(final[d - 1, data : data + blocks, :]) - WORD)
        if first:
            f, high, low = (
                to_float(final[d - 1, data + (i + 1) * blocks : data + (i + 2) * blocks, :])
                for i in range(3)
            )
            cols = cols + (high + low * F32(2.0**-WORD)) * jnp.exp2(f - WORD)
    if first:
        for b in range(blocks):
            weight_ref[b] = F32(1) + cols[b : b + 1, :]

    def finish(b, _):
        total = partial[b]
        for d in range(1, columns):
            value = to_float(final[d - 1, pl.ds(pl.multiple_of(b * seeds, seeds), seeds), :])
            total = total + value * scales[d - 1, pl.ds(b, 1), :]
        inflow_ref[b] = total
        return 0

    lax.fori_loop(0, blocks, finish, 0)
    for d in order:
        for t in others:
            across(d, t, r).wait_send()
    for d in order[:-1]:
        along(d).wait_send()


def trust_kernel(inflow, good_ref, spam_ref, weight_ref, trust_ref, shield_ref, share_ref):
    size = inflow.shape[2]

    def one(b, _):
        trust = F32(0.85) * inflow[b] + F32(0.15) * good_ref[b]
        trust_ref[pl.ds(pl.multiple_of(b * size, size), size), :] = jnp.transpose(trust)
        shield_ref[b] = F32(1) / (F32(1) + trust)
        return 0

    lax.fori_loop(0, inflow.shape[0], one, 0)
    shares(shield_ref, weight_ref, lambda b: spam_ref[b], share_ref)


def pull_kernel(last, *refs):
    if last:
        src_ref, slot_ref, fetched_ref, spam_ref, tiles_ref, out_ref, acc = refs
    else:
        (src_ref, slot_ref, fetched_ref, spam_ref, shield_ref, weight_ref, tiles_ref,
         out_ref, acc) = refs
    step = pl.program_id(0)
    per_step = tiles_ref.shape[0]
    size = acc.shape[2]

    @pl.when(step == 0)
    def _():
        acc[...] = jnp.zeros_like(acc)

    def some(g, _):
        products = []
        for k in range(GROUP):
            n = step * per_step + g * GROUP + k
            products.append(
                lax.dot_general(
                    fetched_ref[slot_ref[n]], tiles_ref[g * GROUP + k], (((1,), (1,)), ((), ())),
                    preferred_element_type=F32,
                )
            )
        for k in range(GROUP):
            acc[src_ref[step * per_step + g * GROUP + k]] += products[k]
        return 0

    lax.fori_loop(0, per_step // GROUP, some, 0)

    @pl.when(step == pl.num_programs(0) - 1)
    def _():
        def distrust(b):
            return F32(0.85) * acc[b] + F32(0.15) * spam_ref[b]

        if last:
            def one(b, _):
                out_ref[pl.ds(pl.multiple_of(b * size, size), size), :] = jnp.transpose(distrust(b))
                return 0

            lax.fori_loop(0, acc.shape[0], one, 0)
        else:
            shares(shield_ref, weight_ref, distrust, out_ref)


def body(columns, tiles, tile_src, tile_slot, slot_block, out_degree, good_seeds, spam_cores):
    tile_count, size, _ = tiles.shape
    hosts = out_degree.shape[0]
    blocks = hosts // size
    seeds = good_seeds.shape[0]
    slots = slot_block.shape[0]
    peers = lax.axis_size(AXES)
    cap = slots // peers
    tail = -(-4 * cap // 16) * 16
    steps = 8
    shape = jax.ShapeDtypeStruct
    vector = (blocks, seeds, size)
    degree = out_degree.reshape(blocks, 1, size)

    rows = peers // columns
    want = lax.all_to_all(
        slot_block.reshape(rows, columns * cap), "row", split_axis=0, concat_axis=0, tiled=True
    )
    good = pl.pallas_call(
        functools.partial(count_seeds, columns),
        out_shape=shape(vector, F32),
        in_specs=[VM],
        out_specs=VM,
    )(good_seeds)

    tile_spec = pl.BlockSpec((tile_count // steps, size, size), lambda i: (i, 0, 0))
    words = shape((peers, cap * size + tail, size), jnp.int16)
    outgoing = pl.pallas_call(
        functools.partial(push_kernel, True, cap),
        grid=(steps,),
        out_shape=words,
        in_specs=[SM, SM, VM, VM, tile_spec],
        out_specs=VM,
        scratch_shapes=[
            pltpu.VMEM((slots, seeds + 16, size), F32),
            pltpu.VMEM((blocks, seeds + 16, size), BF16),
        ],
    )(tile_src, tile_slot, good, degree, tiles)
    def reduce(first, words_in, *rest):
        long = blocks * seeds + blocks * (4 if first else 1)
        outs = (shape(vector, F32), shape((blocks, 1, size), F32), shape(vector, F32))
        return pl.pallas_call(
            functools.partial(reduce_kernel, first, rows, columns, cap),
            out_shape=outs if first else outs[:1],
            in_specs=[SM, VM, VM] if first else [SM, VM],
            out_specs=(VM, VM, VM) if first else (VM,),
            scratch_shapes=[
                pltpu.VMEM((columns, rows, cap * size + tail, size), jnp.int16),
                pltpu.VMEM((rows * cap, blocks, size), F32),
                pltpu.VMEM(vector, F32),
                pltpu.VMEM((blocks, size), F32),
                pltpu.VMEM((columns - 1, blocks, size), F32),
                pltpu.VMEM((columns - 1, long, size), jnp.int16),
                pltpu.VMEM((columns - 1, long, size), jnp.int16),
                pltpu.SemaphoreType.DMA((columns,)),
                pltpu.SemaphoreType.DMA((columns, rows)),
                pltpu.SemaphoreType.DMA((columns, rows)),
                pltpu.SemaphoreType.DMA((columns - 1,)),
                pltpu.SemaphoreType.DMA((columns - 1,)),
            ],
            compiler_params=pltpu.CompilerParams(
                collective_id=1 if first else 2, has_side_effects=True
            ),
        )(want, words_in, *rest)

    inflow, weight, spam = reduce(True, outgoing, spam_cores)
    outgoing = pl.pallas_call(
        functools.partial(push_kernel, False, cap),
        grid=(steps,),
        out_shape=words,
        in_specs=[SM, SM, VM, VM, VM, tile_spec],
        out_specs=VM,
        scratch_shapes=[
            pltpu.VMEM((slots, seeds, size), F32),
            pltpu.VMEM(vector, BF16),
        ],
    )(tile_src, tile_slot, inflow, good, degree, tiles)
    (inflow,) = reduce(False, outgoing)
    fetch = pl.pallas_call(
        functools.partial(fetch_kernel, rows, columns, cap),
        out_shape=shape((slots, seeds, size), BF16),
        in_specs=[SM, VM],
        out_specs=VM,
        scratch_shapes=[
            *[pltpu.VMEM(vector, BF16)] * (2 * columns - 2),
            pltpu.VMEM((rows, columns * cap, seeds, size), BF16),
            pltpu.SemaphoreType.DMA((2 * columns - 2,)),
            pltpu.SemaphoreType.DMA((2 * columns - 2,)),
            pltpu.SemaphoreType.DMA((rows, columns)),
            pltpu.SemaphoreType.DMA((rows, columns)),
        ],
        compiler_params=pltpu.CompilerParams(collective_id=0, has_side_effects=True),
    )
    trust, shield, share = pl.pallas_call(
        trust_kernel,
        out_shape=(shape((hosts, seeds), F32), shape(vector, F32), shape(vector, BF16)),
        in_specs=[VM, VM, VM, VM],
        out_specs=(VM, VM, VM),
    )(inflow, good, spam, weight)
    fetched = fetch(want, share)
    share = pl.pallas_call(
        functools.partial(pull_kernel, False),
        grid=(steps,),
        out_shape=shape(vector, BF16),
        in_specs=[SM, SM, VM, VM, VM, VM, tile_spec],
        out_specs=VM,
        scratch_shapes=[pltpu.VMEM(vector, F32)],
    )(tile_src, tile_slot, fetched, spam, shield, weight, tiles)
    fetched = fetch(want, share)
    distrust = pl.pallas_call(
        functools.partial(pull_kernel, True),
        grid=(steps,),
        out_shape=shape((hosts, seeds), F32),
        in_specs=[SM, SM, VM, VM, tile_spec],
        out_specs=VM,
        scratch_shapes=[pltpu.VMEM(vector, F32)],
    )(tile_src, tile_slot, fetched, spam, tiles)
    return trust, distrust


def solution(mesh):
    in_specs = (
        P(AXES, None, None),
        P(AXES),
        P(AXES),
        P(AXES),
        P(AXES),
        P(None, AXES),
        P(None, AXES),
    )
    out_specs = (P(AXES, None), P(AXES, None))
    return jax.shard_map(
        functools.partial(body, mesh.shape["col"]),
        mesh=mesh, in_specs=in_specs, out_specs=out_specs, check_vma=False,
    )
```
